32 devices in a mesh: parts: 2 (over x), tm: 16 (over z, y, core).
Axes of the slice: x: 2, y: 2, z: 4, core: 2. Of those that a mesh axis runs over, the one named last changes fastest.
Arguments:
- query_states: bfloat16 [32, 384, 768], P(('parts', 'tm')), parts along dimension 0, may hold values from -88 to 88
- key_states: bfloat16 [32, 384, 768], P(('parts', 'tm')), parts along dimension 0, may hold values from -4 to 4
- value_states: bfloat16 [32, 384, 768], P(('parts', 'tm')), parts along dimension 0, may hold values from -40 to 40
- out_weight: bfloat16 [1536, 3072], replicated, may hold values from -0.15625 to 0.15625
Outputs:
- mixed: bfloat16 [6144, 3072], P(('parts', 'tm')), parts along dimension 0
The draws below stay inside these ranges and needn't reach their ends.
There are 2 independent parts, one for each index of `parts`. The reference program is written for one: setup_inputs(seed, part) draws one part's arguments, and reference() takes and returns one part's arrays. A program takes and returns all parts, laid end to end along the dimension named above; an argument that names none is the same for every part. Nothing has to cross between parts.
All inputs are finite; a program needn't handle non-finite values.
Results may differ from the reference program's by a relative error of at most 0.0058.
Values may be sent and summed in bfloat16 or wider, within the bound.
A program may use at most 128 MiB of HBM per device.

```python
import jax
import jax.numpy as jnp
from jax import lax

TCOLS = 4
HEADS = 12
HD = 128
D = 3072
TOK_DEV = 384
TILES = 8
T_TILES = 2
TOKENS = 3072


def to_blocks(grid):
    half_width = grid.shape[2] // 2
    return grid.reshape(TILES, TOK_DEV, 2, half_width).transpose(0, 2, 1, 3).reshape(2 * TILES, TOK_DEV, half_width)


def key_grid(key):
    normal_draw = jax.random.normal(jax.random.fold_in(key, 7), (TILES, TOK_DEV, HEADS * HD), jnp.float32)
    values_out = jnp.clip(normal_draw, -4.0, 4.0)
    sign_draw = jnp.where(jax.random.bernoulli(jax.random.fold_in(key, 13), 0.5, (TILES,)), 4.0, -4.0)
    last_col = HEADS * HD - 1
    pick_row = 5 % TOK_DEV
    values_out = values_out.at[:, pick_row, last_col].set(sign_draw)
    values_out = values_out.at[:, pick_row, last_col - 1].set(-sign_draw)
    return values_out


def draw_key_states(key, part):
    values_out = key_grid(key)
    return to_blocks(values_out).astype(jnp.bfloat16)


def draw_query_states(key, part):
    normal_draw = jax.random.normal(jax.random.fold_in(key, 3), (TILES, TOK_DEV, HEADS * HD), jnp.float32)
    values_out = jnp.clip(normal_draw, -4.0, 4.0)
    return to_blocks(values_out).astype(jnp.bfloat16)


def shard_levels(stream_key, shape, cuts, low, high):
    level = 1.0
    for position, blocks in cuts:
        draws = jax.random.uniform(jax.random.fold_in(jax.random.fold_in(stream_key, 6), position), (blocks,), jnp.float32, low / len(cuts), high / len(cuts))
        level = level * jnp.repeat(jnp.exp(draws), shape[position] // blocks).reshape((-1,) + (1,) * (len(shape) - 1 - position))
    return level


def gaussian(key, dims, scale, most, cuts=(), held_as=jnp.bfloat16):
    loudness = shard_levels(key, dims, cuts, -0.22, 0.18) if cuts else 1.0
    values = jax.random.normal(key, dims, jnp.float32) * scale * loudness
    return jnp.minimum(jnp.maximum(values, -most), most).astype(held_as)


def setup_inputs(seed: int = 0, part: int = 0) -> dict:
    seeds = jax.random.split(jax.random.key(seed), 5)
    own_keys = jax.random.split(jax.random.fold_in(seeds[4], part), 5)
    query_states = draw_query_states(jax.random.fold_in(jax.random.fold_in(seeds[4], part), 71), part)
    key_states = draw_key_states(jax.random.fold_in(jax.random.fold_in(seeds[4], part), 71), part)
    value_states = gaussian(own_keys[2], (2 * TILES, TOK_DEV, HEADS * HD // 2), 8.0, 40.0, ((0, 16),))
    out_weight = gaussian(seeds[3], (HEADS * HD, D), (HEADS * HD) ** -0.5, 0.15625)
    return {"query_states": query_states, "key_states": key_states, "value_states": value_states, "out_weight": out_weight}


masked_score = -1e30


def to_tiles(blocks):
    tile_count = blocks.shape[0] // 2
    half_width = blocks.shape[2]
    return blocks.reshape(tile_count, 2, TOK_DEV, half_width).transpose(0, 2, 1, 3).reshape(tile_count, TOK_DEV, 2 * half_width)


def tile_attention(query_tile, key_window, value_window, key_ok):
    score_scale = HD ** -0.5
    pieces = []
    for head_index in range(HEADS):
        first_col = head_index * HD
        query_head = query_tile[:, first_col:first_col + HD]
        key_head = key_window[:, first_col:first_col + HD]
        value_head = value_window[:, first_col:first_col + HD]
        scores = lax.dot_general(query_head, key_head, (((1,), (1,)), ((), ())), preferred_element_type=jnp.float32) * score_scale
        scores = jnp.where(key_ok[None, :], scores, masked_score)
        row_max = jnp.max(scores, axis=1, keepdims=True)
        exp_scores = jnp.exp(scores - row_max)
        denominator = jnp.sum(exp_scores, axis=1, keepdims=True)
        weights = (exp_scores / denominator).astype(jnp.bfloat16)
        pieces.append(jnp.dot(weights, value_head, preferred_element_type=jnp.float32).astype(jnp.bfloat16))
    return jnp.concatenate(pieces, axis=1)


def reference(query_states, key_states, value_states, out_weight):
    width_all = HEADS * HD
    query_tiles = to_tiles(query_states)
    key_layout = to_tiles(key_states).reshape(T_TILES, TCOLS, TOK_DEV, width_all)
    value_layout = to_tiles(value_states).reshape(T_TILES, TCOLS, TOK_DEV, width_all)
    border = ((1, 1), (1, 1), (0, 0), (0, 0))
    key_padded = jnp.pad(key_layout, border)
    value_padded = jnp.pad(value_layout, border)
    tile_steps = jnp.arange(3, dtype=jnp.int32) - 1
    zero_index = jnp.zeros((), jnp.int32)

    def one_tile(tile_index):
        time_tile = (tile_index // TCOLS).astype(jnp.int32)
        col_tile = (tile_index % TCOLS).astype(jnp.int32)
        starts = (time_tile, col_tile, zero_index, zero_index)
        window_shape = (3, 3, TOK_DEV, width_all)
        key_window = lax.dynamic_slice(key_padded, starts, window_shape).reshape(9 * TOK_DEV, width_all)
        value_window = lax.dynamic_slice(value_padded, starts, window_shape).reshape(9 * TOK_DEV, width_all)
        time_ok = (time_tile + tile_steps >= 0) & (time_tile + tile_steps < T_TILES)
        col_ok = (col_tile + tile_steps >= 0) & (col_tile + tile_steps < TCOLS)
        tile_ok = (time_ok[:, None] & col_ok[None, :]).reshape(9)
        key_ok = jnp.repeat(tile_ok, TOK_DEV)
        query_tile = lax.dynamic_index_in_dim(query_tiles, tile_index, 0, keepdims=False)
        return tile_attention(query_tile, key_window, value_window, key_ok)

    attended = lax.map(one_tile, jnp.arange(TILES, dtype=jnp.int32)).reshape(TOKENS, width_all)
    mixed_rows = jnp.dot(attended, out_weight, preferred_element_type=jnp.float32)
    return mixed_rows.astype(jnp.bfloat16)
```

```python
import functools

import jax
import jax.numpy as jnp
from jax import lax
from jax.experimental import pallas as pl
from jax.experimental.pallas import tpu as pltpu
from jax.sharding import PartitionSpec as P

TCOLS = 4
HD = 128
MESH = pl.DeviceIdType.MESH
LOG2E = 1.4426950408889634

DIRECT_OWN = 0
DIRECT_CORNER = 0
LAG = 3


def slot_of(time_step, col_step):
    return (time_step + 1) * 3 + col_step + 1


def kernel(
    time_count,
    heads,
    q_hbm,
    k_hbm,
    v_hbm,
    w_hbm,
    out_ref,
    q_s,
    kv,
    w_s,
    m_s,
    l_s,
    acc_s,
    outgoing,
    attended,
    load_sem,
    w_sem,
    send_sem,
    recv_sem,
    att_send_sem,
    att_recv_sem,
):
    rows = q_s.shape[1]
    half = rows // 2
    me = lax.axis_index("tm")
    group = lax.rem(me, 2)
    tile = lax.div(me, 2)
    col = lax.rem(tile, TCOLS)
    time = lax.div(tile, TCOLS)
    has_time = {-1: time > 0, 1: time < time_count - 1}
    has_col = {-1: col > 0, 1: col < TCOLS - 1}
    outer = 1 - 2 * lax.rem(col, 2)
    is_edge = jnp.logical_or(col == 0, col == TCOLS - 1)
    is_middle = jnp.logical_not(is_edge)
    outer_device = me + 2 * outer
    middle_device = me - 2 * outer
    relay_device = me + 4 * outer
    across = me + 4 * (1 - 2 * lax.div(col, 2))
    other_core = me + 1 - 2 * group
    own_slot = slot_of(0, 0)

    def load(h):
        columns = pl.ds(h * HD, HD)
        return (
            pltpu.make_async_copy(k_hbm.at[0, :, columns], kv.at[own_slot, h, 0], load_sem.at[0, h]),
            pltpu.make_async_copy(v_hbm.at[0, :, columns], kv.at[own_slot, h, 1], load_sem.at[1, h]),
            pltpu.make_async_copy(q_hbm.at[0, :, columns], q_s.at[h], load_sem.at[2, h]),
        )

    for h in range(heads):
        for copy in load(h):
            copy.start()
    w_copy = pltpu.make_async_copy(w_hbm, w_s, w_sem)
    w_copy.start()

    barrier = pltpu.get_barrier_semaphore()

    def greet(device):
        pl.semaphore_signal(barrier, inc=1, device_id={"tm": device}, device_id_type=MESH)

    greetings = jnp.int32(3)
    greet(other_core)
    greet(across)
    greet(outer_device)
    for step in (-1, 1):
        pl.when(has_time[step])(lambda step=step: greet(me + 2 * TCOLS * step))
        greetings = greetings + has_time[step].astype(jnp.int32)
    pl.when(is_middle)(lambda: greet(middle_device))
    greetings = greetings + is_middle.astype(jnp.int32)
    pl.semaphore_wait(barrier, greetings)

    def transfer(kind, h, source, target, device):
        return pltpu.make_async_remote_copy(
            src_ref=kv.at[source, h],
            dst_ref=kv.at[target, h],
            send_sem=send_sem.at[kind, h],
            recv_sem=recv_sem.at[target, h],
            device_id={"tm": device},
            device_id_type=MESH,
        )

    def arrive(slot, h):
        transfer(0, h, slot, slot, other_core).wait_recv()

    def send_time(step, h):
        return transfer(0 if step < 0 else 1, h, own_slot, slot_of(-step, 0), me + 2 * TCOLS * step)

    def send_outer(step, h):
        return transfer(3 + step, h, slot_of(step, 0), slot_of(step, 0) - outer, outer_device)

    def send_middle(step, h):
        return transfer(6 + step, h, slot_of(step, 0), slot_of(step, 0) + outer, middle_device)

    def send_relay(step, h):
        return transfer(9 + step, h, slot_of(step, 0) + outer, slot_of(step, 0) - outer, relay_device)

    def straight(step, h):
        return h >= heads - (DIRECT_OWN if step == 0 else DIRECT_CORNER)

    def send_att(h):
        return pltpu.make_async_remote_copy(
            src_ref=outgoing.at[h],
            dst_ref=attended.at[group, h],
            send_sem=att_send_sem.at[h],
            recv_sem=att_recv_sem.at[h],
            device_id={"tm": other_core},
            device_id_type=MESH,
        )

    def recv_att(h):
        return pltpu.make_async_remote_copy(
            src_ref=outgoing.at[h],
            dst_ref=attended.at[1 - group, h],
            send_sem=att_send_sem.at[h],
            recv_sem=att_recv_sem.at[h],
            device_id={"tm": other_core},
            device_id_type=MESH,
        )

    for h in range(heads):
        copies = load(h)
        copies[0].wait()
        copies[1].wait()
        for step in (-1, 1):
            pl.when(has_time[step])(lambda step=step, h=h: send_time(step, h).start())
        send_outer(0, h).start()
        if h >= heads - DIRECT_OWN:
            pl.when(is_middle)(lambda h=h: send_middle(0, h).start())

    for h in range(heads):
        load(h)[2].wait()

    exponent_scale = (HD ** (-0.5)) * LOG2E

    def attend(slot, h, first=False):
        scores = lax.dot_general(
            q_s[h], kv[slot, h, 0], (((1,), (1,)), ((), ())), preferred_element_type=jnp.float32
        )
        row_max = jnp.max(scores, axis=1, keepdims=True)
        if not first:
            old_max = m_s[h][:, :1]
            row_max = jnp.maximum(row_max, old_max)
        weights = jnp.exp2((scores - row_max) * exponent_scale)
        total = jnp.sum(weights, axis=1, keepdims=True)
        result = jnp.dot(weights.astype(jnp.bfloat16), kv[slot, h, 1], preferred_element_type=jnp.float32)
        if not first:
            keep = jnp.exp2((old_max - row_max) * exponent_scale)
            total = total + keep * l_s[h][:, :1]
            result = result + keep * acc_s[h]
        m_s[h] = jnp.broadcast_to(row_max, (rows, HD))
        l_s[h] = jnp.broadcast_to(total, (rows, HD))
        acc_s[h] = result

    def finish(h):
        acc_s[h] = acc_s[h] / l_s[h]
        attended[group, h] = acc_s[h, pl.ds(pl.multiple_of(group * half, 16), half), :].astype(jnp.bfloat16)
        outgoing[h] = acc_s[h, pl.ds(pl.multiple_of((1 - group) * half, 16), half), :].astype(jnp.bfloat16)

    @pl.loop(0, heads + LAG)
    def _(i):
        @pl.when(i < heads)
        def _():
            for step in (-1, 1):

                @pl.when(has_time[step])
                def _():
                    arrive(slot_of(step, 0), i)
                    send_outer(step, i).start()
                    if DIRECT_CORNER:
                        pl.when(jnp.logical_and(is_middle, straight(step, i)))(
                            lambda: send_middle(step, i).start()
                        )

            @pl.when(is_edge)
            def _():
                arrive(own_slot + outer, i)
                pl.when(jnp.logical_not(straight(0, i)))(lambda: send_relay(0, i).start())

        back = i - 1

        @pl.when(jnp.logical_and(jnp.logical_and(back >= 0, back < heads), is_edge))
        def _():
            for step in (-1, 1):

                @pl.when(has_time[step])
                def _():
                    arrive(slot_of(step, 0) + outer, back)
                    pl.when(jnp.logical_not(straight(step, back)))(lambda: send_relay(step, back).start())

        @pl.when(i < heads)
        def _():
            attend(own_slot, i, first=True)
            for step in (-1, 1):
                pl.when(has_time[step])(lambda: attend(slot_of(step, 0), i))

        @pl.when(jnp.logical_and(back >= 0, back < heads))
        def _():
            pl.when(is_middle)(lambda: arrive(own_slot + outer, back))
            attend(own_slot + outer, back)
            for step in (-1, 1):

                @pl.when(has_time[step])
                def _():
                    pl.when(is_middle)(lambda: arrive(slot_of(step, 0) + outer, back))
                    attend(slot_of(step, 0) + outer, back)

        last = i - LAG

        @pl.when(last >= 1)
        def _():
            send_att(last - 1).start()

        @pl.when(last >= 0)
        def _():
            @pl.when(is_middle)
            def _():
                arrive(own_slot - outer, last)
                attend(own_slot - outer, last)
                for step in (-1, 1):

                    @pl.when(has_time[step])
                    def _():
                        arrive(slot_of(step, 0) - outer, last)
                        attend(slot_of(step, 0) - outer, last)

            finish(last)

    send_att(heads - 1).start()
    w_copy.wait()

    for h in range(heads):
        recv_att(h).wait_recv()

    width = out_ref.shape[1]
    chunk = 512
    lhs = jnp.concatenate([attended[part, h] for part in range(2) for h in range(heads)], axis=1)

    @pl.loop(0, width // chunk)
    def _(n):
        columns = pl.ds(pl.multiple_of(n * chunk, chunk), chunk)
        out_ref[:, columns] = jnp.dot(lhs, w_s[:, columns], preferred_element_type=jnp.float32).astype(
            out_ref.dtype
        )

    @pl.loop(0, heads)
    def _(h):
        send_att(h).wait_send()
        send_outer(0, h).wait_send()
        if DIRECT_OWN:
            pl.when(jnp.logical_and(is_middle, straight(0, h)))(lambda: send_middle(0, h).wait_send())
        pl.when(jnp.logical_and(is_edge, jnp.logical_not(straight(0, h))))(
            lambda: send_relay(0, h).wait_send()
        )
        for step in (-1, 1):

            @pl.when(has_time[step])
            def _():
                send_time(step, h).wait_send()
                send_outer(step, h).wait_send()
                if DIRECT_CORNER:
                    pl.when(jnp.logical_and(is_middle, straight(step, h)))(
                        lambda: send_middle(step, h).wait_send()
                    )
                pl.when(jnp.logical_and(is_edge, jnp.logical_not(straight(step, h))))(
                    lambda: send_relay(step, h).wait_send()
                )


def per_device(query_states, key_states, value_states, out_weight):
    rows, half_width = query_states.shape[1:]
    heads = half_width // HD
    depth, width = out_weight.shape
    time_count = lax.axis_size("tm") // (2 * TCOLS)
    return pl.pallas_call(
        functools.partial(kernel, time_count, heads),
        out_shape=jax.ShapeDtypeStruct((rows // 2, width), jnp.bfloat16),
        in_specs=[pl.BlockSpec(memory_space=pl.ANY)] * 4,
        out_specs=pl.BlockSpec(memory_space=pltpu.VMEM),
        scratch_shapes=[
            pltpu.VMEM((heads, rows, HD), jnp.bfloat16),
            pltpu.VMEM((9, heads, 2, rows, HD), jnp.bfloat16),
            pltpu.VMEM((depth, width), jnp.bfloat16),
            pltpu.VMEM((heads, rows, HD), jnp.float32),
            pltpu.VMEM((heads, rows, HD), jnp.float32),
            pltpu.VMEM((heads, rows, HD), jnp.float32),
            pltpu.VMEM((heads, rows // 2, HD), jnp.bfloat16),
            pltpu.VMEM((2, heads, rows // 2, HD), jnp.bfloat16),
            pltpu.SemaphoreType.DMA((3, heads)),
            pltpu.SemaphoreType.DMA,
            pltpu.SemaphoreType.DMA((11, heads)),
            pltpu.SemaphoreType.DMA((9, heads)),
            pltpu.SemaphoreType.DMA((heads,)),
            pltpu.SemaphoreType.DMA((heads,)),
        ],
        compiler_params=pltpu.CompilerParams(
            collective_id=0, has_side_effects=True, vmem_limit_bytes=56 * 1024 * 1024
        ),
    )(query_states, key_states, value_states, out_weight)


def solution(mesh):
    in_specs = (
        P(("parts", "tm"), None, None),
        P(("parts", "tm"), None, None),
        P(("parts", "tm"), None, None),
        P(),
    )
    out_specs = P(("parts", "tm"), None)
    return jax.shard_map(
        per_device, mesh=mesh, in_specs=in_specs, out_specs=out_specs, check_vma=False
    )
```

```python
import functools

import jax
import jax.numpy as jnp
from jax import lax
from jax.experimental import pallas as pl
from jax.experimental.pallas import tpu as pltpu
from jax.sharding import PartitionSpec as P

TCOLS = 4
HD = 128
MESH = pl.DeviceIdType.MESH
LOG2E = 1.4426950408889634

DIRECT_OWN = 2
DIRECT_CORNER = 1
LAG = 3


def slot_of(time_step, col_step):
    return (time_step + 1) * 3 + col_step + 1


def kernel(
    time_count,
    heads,
    q_hbm,
    k_hbm,
    v_hbm,
    w_hbm,
    out_ref,
    q_s,
    kv,
    w_s,
    m_s,
    l_s,
    acc_s,
    outgoing,
    attended,
    load_sem,
    w_sem,
    send_sem,
    recv_sem,
    att_send_sem,
    att_recv_sem,
):
    rows = q_s.shape[1]
    half = rows // 2
    me = lax.axis_index("tm")
    group = lax.rem(me, 2)
    tile = lax.div(me, 2)
    col = lax.rem(tile, TCOLS)
    time = lax.div(tile, TCOLS)
    has_time = {-1: time > 0, 1: time < time_count - 1}
    has_col = {-1: col > 0, 1: col < TCOLS - 1}
    outer = 1 - 2 * lax.rem(col, 2)
    is_edge = jnp.logical_or(col == 0, col == TCOLS - 1)
    is_middle = jnp.logical_not(is_edge)
    outer_device = me + 2 * outer
    middle_device = me - 2 * outer
    relay_device = me + 4 * outer
    across = me + 4 * (1 - 2 * lax.div(col, 2))
    other_core = me + 1 - 2 * group
    own_slot = slot_of(0, 0)

    def load(h):
        columns = pl.ds(h * HD, HD)
        return (
            pltpu.make_async_copy(k_hbm.at[0, :, columns], kv.at[own_slot, h, 0], load_sem.at[0, h]),
            pltpu.make_async_copy(v_hbm.at[0, :, columns], kv.at[own_slot, h, 1], load_sem.at[1, h]),
            pltpu.make_async_copy(q_hbm.at[0, :, columns], q_s.at[h], load_sem.at[2, h]),
        )

    for h in range(heads):
        for copy in load(h):
            copy.start()
    w_copy = pltpu.make_async_copy(w_hbm, w_s, w_sem)
    w_copy.start()

    barrier = pltpu.get_barrier_semaphore()

    def greet(device):
        pl.semaphore_signal(barrier, inc=1, device_id={"tm": device}, device_id_type=MESH)

    greetings = jnp.int32(3)
    greet(other_core)
    greet(across)
    greet(outer_device)
    for step in (-1, 1):
        pl.when(has_time[step])(lambda step=step: greet(me + 2 * TCOLS * step))
        greetings = greetings + has_time[step].astype(jnp.int32)
    pl.when(is_middle)(lambda: greet(middle_device))
    greetings = greetings + is_middle.astype(jnp.int32)
    pl.semaphore_wait(barrier, greetings)

    def transfer(kind, h, source, target, device):
        return pltpu.make_async_remote_copy(
            src_ref=kv.at[source, h],
            dst_ref=kv.at[target, h],
            send_sem=send_sem.at[kind, h],
            recv_sem=recv_sem.at[target, h],
            device_id={"tm": device},
            device_id_type=MESH,
        )

    def arrive(slot, h):
        transfer(0, h, slot, slot, other_core).wait_recv()

    def send_time(step, h):
        return transfer(0 if step < 0 else 1, h, own_slot, slot_of(-step, 0), me + 2 * TCOLS * step)

    def send_outer(step, h):
        return transfer(3 + step, h, slot_of(step, 0), slot_of(step, 0) - outer, outer_device)

    def send_middle(step, h):
        return transfer(6 + step, h, slot_of(step, 0), slot_of(step, 0) + outer, middle_device)

    def send_relay(step, h):
        return transfer(9 + step, h, slot_of(step, 0) + outer, slot_of(step, 0) - outer, relay_device)

    def straight(step, h):
        return h >= heads - (DIRECT_OWN if step == 0 else DIRECT_CORNER)

    def send_att(h):
        return pltpu.make_async_remote_copy(
            src_ref=outgoing.at[h],
            dst_ref=attended.at[group, h],
            send_sem=att_send_sem.at[h],
            recv_sem=att_recv_sem.at[h],
            device_id={"tm": other_core},
            device_id_type=MESH,
        )

    def recv_att(h):
        return pltpu.make_async_remote_copy(
            src_ref=outgoing.at[h],
            dst_ref=attended.at[1 - group, h],
            send_sem=att_send_sem.at[h],
            recv_sem=att_recv_sem.at[h],
            device_id={"tm": other_core},
            device_id_type=MESH,
        )

    for h in range(heads):
        copies = load(h)
        copies[0].wait()
        copies[1].wait()
        for step in (-1, 1):
            pl.when(has_time[step])(lambda step=step, h=h: send_time(step, h).start())
        send_outer(0, h).start()
        if h >= heads - DIRECT_OWN:
            pl.when(is_middle)(lambda h=h: send_middle(0, h).start())

    for h in range(heads):
        load(h)[2].wait()

    exponent_scale = (HD ** (-0.5)) * LOG2E

    def attend(slot, h, first=False):
        scores = lax.dot_general(
            q_s[h], kv[slot, h, 0], (((1,), (1,)), ((), ())), preferred_element_type=jnp.float32
        )
        row_max = jnp.max(scores, axis=1, keepdims=True)
        if not first:
            old_max = m_s[h][:, :1]
            row_max = jnp.maximum(row_max, old_max)
        weights = jnp.exp2((scores - row_max) * exponent_scale)
        total = jnp.sum(weights, axis=1, keepdims=True)
        result = jnp.dot(weights.astype(jnp.bfloat16), kv[slot, h, 1], preferred_element_type=jnp.float32)
        if not first:
            keep = jnp.exp2((old_max - row_max) * exponent_scale)
            total = total + keep * l_s[h][:, :1]
            result = result + keep * acc_s[h]
        m_s[h] = jnp.broadcast_to(row_max, (rows, HD))
        l_s[h] = jnp.broadcast_to(total, (rows, HD))
        acc_s[h] = result

    def finish(h):
        acc_s[h] = acc_s[h] / l_s[h]
        attended[group, h] = acc_s[h, pl.ds(pl.multiple_of(group * half, 16), half), :].astype(jnp.bfloat16)
        outgoing[h] = acc_s[h, pl.ds(pl.multiple_of((1 - group) * half, 16), half), :].astype(jnp.bfloat16)

    @pl.loop(0, heads + LAG)
    def _(i):
        @pl.when(i < heads)
        def _():
            for step in (-1, 1):

                @pl.when(has_time[step])
                def _():
                    arrive(slot_of(step, 0), i)
                    send_outer(step, i).start()
                    if DIRECT_CORNER:
                        pl.when(jnp.logical_and(is_middle, straight(step, i)))(
                            lambda: send_middle(step, i).start()
                        )

            @pl.when(is_edge)
            def _():
                arrive(own_slot + outer, i)
                pl.when(jnp.logical_not(straight(0, i)))(lambda: send_relay(0, i).start())

        back = i - 1

        @pl.when(jnp.logical_and(jnp.logical_and(back >= 0, back < heads), is_edge))
        def _():
            for step in (-1, 1):

                @pl.when(has_time[step])
                def _():
                    arrive(slot_of(step, 0) + outer, back)
                    pl.when(jnp.logical_not(straight(step, back)))(lambda: send_relay(step, back).start())

        @pl.when(i < heads)
        def _():
            attend(own_slot, i, first=True)
            for step in (-1, 1):
                pl.when(has_time[step])(lambda: attend(slot_of(step, 0), i))

        @pl.when(jnp.logical_and(back >= 0, back < heads))
        def _():
            pl.when(is_middle)(lambda: arrive(own_slot + outer, back))
            attend(own_slot + outer, back)
            for step in (-1, 1):

                @pl.when(has_time[step])
                def _():
                    pl.when(is_middle)(lambda: arrive(slot_of(step, 0) + outer, back))
                    attend(slot_of(step, 0) + outer, back)

        last = i - LAG

        @pl.when(last >= 1)
        def _():
            send_att(last - 1).start()

        @pl.when(last >= 0)
        def _():
            @pl.when(is_middle)
            def _():
                arrive(own_slot - outer, last)
                attend(own_slot - outer, last)
                for step in (-1, 1):

                    @pl.when(has_time[step])
                    def _():
                        arrive(slot_of(step, 0) - outer, last)
                        attend(slot_of(step, 0) - outer, last)

            finish(last)

    send_att(heads - 1).start()
    w_copy.wait()

    for h in range(heads):
        recv_att(h).wait_recv()

    width = out_ref.shape[1]
    chunk = 512
    lhs = jnp.concatenate([attended[part, h] for part in range(2) for h in range(heads)], axis=1)

    @pl.loop(0, width // chunk)
    def _(n):
        columns = pl.ds(pl.multiple_of(n * chunk, chunk), chunk)
        out_ref[:, columns] = jnp.dot(lhs, w_s[:, columns], preferred_element_type=jnp.float32).astype(
            out_ref.dtype
        )

    @pl.loop(0, heads)
    def _(h):
        send_att(h).wait_send()
        send_outer(0, h).wait_send()
        if DIRECT_OWN:
            pl.when(jnp.logical_and(is_middle, straight(0, h)))(lambda: send_middle(0, h).wait_send())
        pl.when(jnp.logical_and(is_edge, jnp.logical_not(straight(0, h))))(
            lambda: send_relay(0, h).wait_send()
        )
        for step in (-1, 1):

            @pl.when(has_time[step])
            def _():
                send_time(step, h).wait_send()
                send_outer(step, h).wait_send()
                if DIRECT_CORNER:
                    pl.when(jnp.logical_and(is_middle, straight(step, h)))(
                        lambda: send_middle(step, h).wait_send()
                    )
                pl.when(jnp.logical_and(is_edge, jnp.logical_not(straight(step, h))))(
                    lambda: send_relay(step, h).wait_send()
                )


def per_device(query_states, key_states, value_states, out_weight):
    rows, half_width = query_states.shape[1:]
    heads = half_width // HD
    depth, width = out_weight.shape
    time_count = lax.axis_size("tm") // (2 * TCOLS)
    return pl.pallas_call(
        functools.partial(kernel, time_count, heads),
        out_shape=jax.ShapeDtypeStruct((rows // 2, width), jnp.bfloat16),
        in_specs=[pl.BlockSpec(memory_space=pl.ANY)] * 4,
        out_specs=pl.BlockSpec(memory_space=pltpu.VMEM),
        scratch_shapes=[
            pltpu.VMEM((heads, rows, HD), jnp.bfloat16),
            pltpu.VMEM((9, heads, 2, rows, HD), jnp.bfloat16),
            pltpu.VMEM((depth, width), jnp.bfloat16),
            pltpu.VMEM((heads, rows, HD), jnp.float32),
            pltpu.VMEM((heads, rows, HD), jnp.float32),
            pltpu.VMEM((heads, rows, HD), jnp.float32),
            pltpu.VMEM((heads, rows // 2, HD), jnp.bfloat16),
            pltpu.VMEM((2, heads, rows // 2, HD), jnp.bfloat16),
            pltpu.SemaphoreType.DMA((3, heads)),
            pltpu.SemaphoreType.DMA,
            pltpu.SemaphoreType.DMA((11, heads)),
            pltpu.SemaphoreType.DMA((9, heads)),
            pltpu.SemaphoreType.DMA((heads,)),
            pltpu.SemaphoreType.DMA((heads,)),
        ],
        compiler_params=pltpu.CompilerParams(
            collective_id=0, has_side_effects=True, vmem_limit_bytes=56 * 1024 * 1024
        ),
    )(query_states, key_states, value_states, out_weight)


def solution(mesh):
    in_specs = (
        P(("parts", "tm"), None, None),
        P(("parts", "tm"), None, None),
        P(("parts", "tm"), None, None),
        P(),
    )
    out_specs = P(("parts", "tm"), None)
    return jax.shard_map(
        per_device, mesh=mesh, in_specs=in_specs, out_specs=out_specs, check_vma=False
    )
```

```python
import functools

import jax
import jax.numpy as jnp
from jax import lax
from jax.experimental import pallas as pl
from jax.experimental.pallas import tpu as pltpu
from jax.sharding import PartitionSpec as P

TCOLS = 4
HD = 128
MESH = pl.DeviceIdType.MESH
LOG2E = 1.4426950408889634

DIRECT_OWN = 2
DIRECT_CORNER = 1
AHEAD = 2
LAG_TIME = 2
LAG_CORNER = 3
LAG_MIDDLE = 5


def slot_of(time_step, col_step):
    return (time_step + 1) * 3 + col_step + 1


def kernel(
    time_count,
    heads,
    q_hbm,
    k_hbm,
    v_hbm,
    w_hbm,
    out_ref,
    q_s,
    kv,
    w_s,
    m_s,
    l_s,
    acc_s,
    outgoing,
    attended,
    load_sem,
    w_sem,
    send_sem,
    recv_sem,
    att_send_sem,
    att_recv_sem,
):
    rows = q_s.shape[1]
    half = rows // 2
    me = lax.axis_index("tm")
    group = lax.rem(me, 2)
    tile = lax.div(me, 2)
    col = lax.rem(tile, TCOLS)
    time = lax.div(tile, TCOLS)
    has_time = {-1: time > 0, 1: time < time_count - 1}
    has_col = {-1: col > 0, 1: col < TCOLS - 1}
    outer = 1 - 2 * lax.rem(col, 2)
    is_edge = jnp.logical_or(col == 0, col == TCOLS - 1)
    is_middle = jnp.logical_not(is_edge)
    outer_device = me + 2 * outer
    middle_device = me - 2 * outer
    relay_device = me + 4 * outer
    other_core = me + 1 - 2 * group
    own_slot = slot_of(0, 0)
    stride = TCOLS
    has_hop = {-1: tile >= stride // 2, 1: tile + stride // 2 < time_count * TCOLS}
    is_hop = jnp.logical_and(has_hop[-1], has_hop[1])

    def hop_slot(step):
        return 9 if step < 0 else 10

    def load(h):
        columns = pl.ds(pl.multiple_of(h * HD, HD), HD)
        return (
            pltpu.make_async_copy(k_hbm.at[0, :, columns], kv.at[own_slot, h, 0], load_sem.at[0, h]),
            pltpu.make_async_copy(v_hbm.at[0, :, columns], kv.at[own_slot, h, 1], load_sem.at[1, h]),
            pltpu.make_async_copy(q_hbm.at[0, :, columns], q_s.at[h], load_sem.at[2, h]),
        )

    for h in range(heads):
        for copy in load(jnp.int32(h)):
            copy.start()
    w_copy = pltpu.make_async_copy(w_hbm, w_s, w_sem)
    w_copy.start()

    barrier = pltpu.get_barrier_semaphore()

    def greet(device):
        pl.semaphore_signal(barrier, inc=1, device_id={"tm": device}, device_id_type=MESH)

    greetings = jnp.int32(2)
    greet(other_core)
    greet(outer_device)
    for step in (-1, 1):
        pl.when(has_hop[step])(lambda step=step: greet(me + stride * step))
        greetings = greetings + has_hop[step].astype(jnp.int32)
    pl.when(is_middle)(lambda: greet(middle_device))
    greetings = greetings + is_middle.astype(jnp.int32)
    pl.semaphore_wait(barrier, greetings)

    def transfer(kind, h, source, target, device):
        return pltpu.make_async_remote_copy(
            src_ref=kv.at[source, h],
            dst_ref=kv.at[target, h],
            send_sem=send_sem.at[kind, h],
            recv_sem=recv_sem.at[target, h],
            device_id={"tm": device},
            device_id_type=MESH,
        )

    def arrive(slot, h):
        transfer(0, h, slot, slot, other_core).wait_recv()

    def send_time(step, h):
        return transfer(0 if step < 0 else 1, h, own_slot, hop_slot(step), me + stride * step)

    def send_hop(step, h):
        return transfer(11 if step < 0 else 12, h, hop_slot(step), slot_of(-step, 0), me + stride * step)

    def send_outer(step, h):
        return transfer(3 + step, h, slot_of(step, 0), slot_of(step, 0) - outer, outer_device)

    def send_middle(step, h):
        return transfer(6 + step, h, slot_of(step, 0), slot_of(step, 0) + outer, middle_device)

    def send_relay(step, h):
        return transfer(9 + step, h, slot_of(step, 0) + outer, slot_of(step, 0) - outer, relay_device)

    def straight(step, h):
        return h >= heads - (DIRECT_OWN if step == 0 else DIRECT_CORNER)

    def send_att(h):
        return pltpu.make_async_remote_copy(
            src_ref=outgoing.at[h],
            dst_ref=attended.at[group, h],
            send_sem=att_send_sem.at[h],
            recv_sem=att_recv_sem.at[h],
            device_id={"tm": other_core},
            device_id_type=MESH,
        )

    def recv_att(h):
        return pltpu.make_async_remote_copy(
            src_ref=outgoing.at[h],
            dst_ref=attended.at[1 - group, h],
            send_sem=att_send_sem.at[h],
            recv_sem=att_recv_sem.at[h],
            device_id={"tm": other_core},
            device_id_type=MESH,
        )

    def send_own(h):
        for copy in load(h):
            copy.wait()
        for step in (-1, 1):
            pl.when(has_time[step])(lambda step=step: send_time(step, h).start())
        send_outer(0, h).start()
        if DIRECT_OWN:
            pl.when(jnp.logical_and(is_middle, straight(0, h)))(lambda: send_middle(0, h).start())

    for h in range(AHEAD):
        send_own(jnp.int32(h))

    exponent_scale = (HD ** (-0.5)) * LOG2E

    def attend(slot, h, first=False):
        scores = lax.dot_general(
            q_s[h], kv[slot, h, 0], (((1,), (1,)), ((), ())), preferred_element_type=jnp.float32
        )
        row_max = jnp.max(scores, axis=1, keepdims=True)
        if not first:
            old_max = m_s[h][:, :1]
            row_max = jnp.maximum(row_max, old_max)
        weights = jnp.exp2((scores - row_max) * exponent_scale)
        total = jnp.sum(weights, axis=1, keepdims=True)
        result = jnp.dot(weights.astype(jnp.bfloat16), kv[slot, h, 1], preferred_element_type=jnp.float32)
        if not first:
            keep = jnp.exp2((old_max - row_max) * exponent_scale)
            total = total + keep * l_s[h][:, :1]
            result = result + keep * acc_s[h]
        m_s[h] = jnp.broadcast_to(row_max, (rows, HD))
        l_s[h] = jnp.broadcast_to(total, (rows, HD))
        acc_s[h] = result

    def finish(h):
        acc_s[h] = acc_s[h] / l_s[h]
        attended[group, h] = acc_s[h, pl.ds(pl.multiple_of(group * half, 16), half), :].astype(jnp.bfloat16)
        outgoing[h] = acc_s[h, pl.ds(pl.multiple_of((1 - group) * half, 16), half), :].astype(jnp.bfloat16)

    def ready(h):
        return jnp.logical_and(h >= 0, h < heads)

    @pl.loop(0, heads + LAG_MIDDLE)
    def _(i):
        pl.when(i + AHEAD < heads)(lambda: send_own(i + AHEAD))

        @pl.when(jnp.logical_and(i < heads, is_edge))
        def _():
            arrive(own_slot + outer, i)
            pl.when(jnp.logical_not(straight(0, i)))(lambda: send_relay(0, i).start())

        @pl.when(jnp.logical_and(i < heads, is_hop))
        def _():
            for step in (-1, 1):
                arrive(hop_slot(step), i)
                send_hop(step, i).start()

        crossed = i - LAG_TIME

        @pl.when(ready(crossed))
        def _():
            for step in (-1, 1):

                @pl.when(has_time[step])
                def _():
                    arrive(slot_of(step, 0), crossed)
                    send_outer(step, crossed).start()
                    if DIRECT_CORNER:
                        pl.when(jnp.logical_and(is_middle, straight(step, crossed)))(
                            lambda: send_middle(step, crossed).start()
                        )

        back = i - LAG_CORNER

        @pl.when(jnp.logical_and(ready(back), is_edge))
        def _():
            for step in (-1, 1):

                @pl.when(has_time[step])
                def _():
                    arrive(slot_of(step, 0) + outer, back)
                    pl.when(jnp.logical_not(straight(step, back)))(lambda: send_relay(step, back).start())

        pl.when(i < heads)(lambda: attend(own_slot, i, first=True))

        @pl.when(ready(crossed))
        def _():
            for step in (-1, 1):
                pl.when(has_time[step])(lambda: attend(slot_of(step, 0), crossed))

        @pl.when(ready(back))
        def _():
            pl.when(is_middle)(lambda: arrive(own_slot + outer, back))
            attend(own_slot + outer, back)
            for step in (-1, 1):

                @pl.when(has_time[step])
                def _():
                    pl.when(is_middle)(lambda: arrive(slot_of(step, 0) + outer, back))
                    attend(slot_of(step, 0) + outer, back)

        last = i - LAG_MIDDLE

        @pl.when(last >= 1)
        def _():
            send_att(last - 1).start()

        @pl.when(last >= 0)
        def _():
            @pl.when(is_middle)
            def _():
                arrive(own_slot - outer, last)
                attend(own_slot - outer, last)
                for step in (-1, 1):

                    @pl.when(has_time[step])
                    def _():
                        arrive(slot_of(step, 0) - outer, last)
                        attend(slot_of(step, 0) - outer, last)

            finish(last)

    send_att(heads - 1).start()
    w_copy.wait()

    for h in range(heads):
        recv_att(h).wait_recv()

    width = out_ref.shape[1]
    chunk = 512
    lhs = jnp.concatenate([attended[part, h] for part in range(2) for h in range(heads)], axis=1)

    @pl.loop(0, width // chunk)
    def _(n):
        columns = pl.ds(pl.multiple_of(n * chunk, chunk), chunk)
        out_ref[:, columns] = jnp.dot(lhs, w_s[:, columns], preferred_element_type=jnp.float32).astype(
            out_ref.dtype
        )

    @pl.loop(0, heads)
    def _(h):
        send_att(h).wait_send()
        send_outer(0, h).wait_send()

        @pl.when(is_hop)
        def _():
            for step in (-1, 1):
                send_hop(step, h).wait_send()

        if DIRECT_OWN:
            pl.when(jnp.logical_and(is_middle, straight(0, h)))(lambda: send_middle(0, h).wait_send())
        pl.when(jnp.logical_and(is_edge, jnp.logical_not(straight(0, h))))(
            lambda: send_relay(0, h).wait_send()
        )
        for step in (-1, 1):

            @pl.when(has_time[step])
            def _():
                send_time(step, h).wait_send()
                send_outer(step, h).wait_send()
                if DIRECT_CORNER:
                    pl.when(jnp.logical_and(is_middle, straight(step, h)))(
                        lambda: send_middle(step, h).wait_send()
                    )
                pl.when(jnp.logical_and(is_edge, jnp.logical_not(straight(step, h))))(
                    lambda: send_relay(step, h).wait_send()
                )


def per_device(query_states, key_states, value_states, out_weight):
    rows, half_width = query_states.shape[1:]
    heads = half_width // HD
    depth, width = out_weight.shape
    time_count = lax.axis_size("tm") // (2 * TCOLS)
    return pl.pallas_call(
        functools.partial(kernel, time_count, heads),
        out_shape=jax.ShapeDtypeStruct((rows // 2, width), jnp.bfloat16),
        in_specs=[pl.BlockSpec(memory_space=pl.ANY)] * 4,
        out_specs=pl.BlockSpec(memory_space=pltpu.VMEM),
        scratch_shapes=[
            pltpu.VMEM((heads, rows, HD), jnp.bfloat16),
            pltpu.VMEM((11, heads, 2, rows, HD), jnp.bfloat16),
            pltpu.VMEM((depth, width), jnp.bfloat16),
            pltpu.VMEM((heads, rows, HD), jnp.float32),
            pltpu.VMEM((heads, rows, HD), jnp.float32),
            pltpu.VMEM((heads, rows, HD), jnp.float32),
            pltpu.VMEM((heads, rows // 2, HD), jnp.bfloat16),
            pltpu.VMEM((2, heads, rows // 2, HD), jnp.bfloat16),
            pltpu.SemaphoreType.DMA((3, heads)),
            pltpu.SemaphoreType.DMA,
            pltpu.SemaphoreType.DMA((13, heads)),
            pltpu.SemaphoreType.DMA((11, heads)),
            pltpu.SemaphoreType.DMA((heads,)),
            pltpu.SemaphoreType.DMA((heads,)),
        ],
        compiler_params=pltpu.CompilerParams(
            collective_id=0, has_side_effects=True, vmem_limit_bytes=56 * 1024 * 1024
        ),
    )(query_states, key_states, value_states, out_weight)


def solution(mesh):
    in_specs = (
        P(("parts", "tm"), None, None),
        P(("parts", "tm"), None, None),
        P(("parts", "tm"), None, None),
        P(),
    )
    out_specs = P(("parts", "tm"), None)
    return jax.shard_map(
        per_device, mesh=mesh, in_specs=in_specs, out_specs=out_specs, check_vma=False
    )
```

```python
import functools

import jax
import jax.numpy as jnp
from jax import lax
from jax.experimental import pallas as pl
from jax.experimental.pallas import tpu as pltpu
from jax.sharding import PartitionSpec as P

TCOLS = 4
HD = 128
MESH = pl.DeviceIdType.MESH
LOG2E = 1.4426950408889634

DIRECT_OWN = 2
DIRECT_CORNER = 1
AHEAD = 2
LAG_TIME = 2
LAG_CORNER = 3
LAG_MIDDLE = 5


def slot_of(time_step, col_step):
    return (time_step + 1) * 3 + col_step + 1


def kernel(
    time_count,
    heads,
    q_hbm,
    k_hbm,
    v_hbm,
    w_hbm,
    out_ref,
    q_s,
    kv,
    w_s,
    m_s,
    l_s,
    acc_s,
    outgoing,
    attended,
    load_sem,
    w_sem,
    send_sem,
    recv_sem,
    att_send_sem,
    att_recv_sem,
):
    rows = q_s.shape[1]
    half = rows // 2
    me = lax.axis_index("tm")
    group = lax.rem(me, 2)
    tile = lax.div(me, 2)
    col = lax.rem(tile, TCOLS)
    time = lax.div(tile, TCOLS)
    has_time = {-1: time > 0, 1: time < time_count - 1}
    has_col = {-1: col > 0, 1: col < TCOLS - 1}
    outer = 1 - 2 * lax.rem(col, 2)
    is_edge = jnp.logical_or(col == 0, col == TCOLS - 1)
    is_middle = jnp.logical_not(is_edge)
    outer_device = me + 2 * outer
    middle_device = me - 2 * outer
    relay_device = me + 4 * outer
    other_core = me + 1 - 2 * group
    own_slot = slot_of(0, 0)
    stride = TCOLS
    has_hop = {-1: tile >= stride // 2, 1: tile + stride // 2 < time_count * TCOLS}
    is_hop = jnp.logical_and(has_hop[-1], has_hop[1])

    def hop_slot(step):
        return 9 if step < 0 else 10

    def load(h):
        columns = pl.ds(pl.multiple_of(h * HD, HD), HD)
        return (
            pltpu.make_async_copy(k_hbm.at[0, :, columns], kv.at[own_slot, h, 0], load_sem.at[0, h]),
            pltpu.make_async_copy(v_hbm.at[0, :, columns], kv.at[own_slot, h, 1], load_sem.at[1, h]),
            pltpu.make_async_copy(q_hbm.at[0, :, columns], q_s.at[h], load_sem.at[2, h]),
        )

    for h in range(heads):
        for copy in load(jnp.int32(h)):
            copy.start()
    w_copy = pltpu.make_async_copy(w_hbm, w_s, w_sem)
    w_copy.start()

    barrier = pltpu.get_barrier_semaphore()

    def greet(device):
        pl.semaphore_signal(barrier, inc=1, device_id={"tm": device}, device_id_type=MESH)

    greetings = jnp.int32(2)
    greet(other_core)
    greet(outer_device)
    for step in (-1, 1):
        pl.when(has_hop[step])(lambda step=step: greet(me + stride * step))
        greetings = greetings + has_hop[step].astype(jnp.int32)
    pl.when(is_middle)(lambda: greet(middle_device))
    greetings = greetings + is_middle.astype(jnp.int32)
    pl.semaphore_wait(barrier, greetings)

    def transfer(kind, h, source, target, device):
        return pltpu.make_async_remote_copy(
            src_ref=kv.at[source, h],
            dst_ref=kv.at[target, h],
            send_sem=send_sem.at[kind, h],
            recv_sem=recv_sem.at[target, h],
            device_id={"tm": device},
            device_id_type=MESH,
        )

    def arrive(slot, h):
        transfer(0, h, slot, slot, other_core).wait_recv()

    def send_time(step, h):
        return transfer(0 if step < 0 else 1, h, own_slot, hop_slot(step), me + stride * step)

    def send_hop(step, h):
        return transfer(11 if step < 0 else 12, h, hop_slot(step), slot_of(-step, 0), me + stride * step)

    def send_outer(step, h):
        return transfer(3 + step, h, slot_of(step, 0), slot_of(step, 0) - outer, outer_device)

    def send_middle(step, h):
        return transfer(6 + step, h, slot_of(step, 0), slot_of(step, 0) + outer, middle_device)

    def send_relay(step, h):
        return transfer(9 + step, h, slot_of(step, 0) + outer, slot_of(step, 0) - outer, relay_device)

    def straight(step, h):
        return h >= heads - (DIRECT_OWN if step == 0 else DIRECT_CORNER)

    def send_att(h):
        return pltpu.make_async_remote_copy(
            src_ref=outgoing.at[h],
            dst_ref=attended.at[group, h],
            send_sem=att_send_sem.at[h],
            recv_sem=att_recv_sem.at[h],
            device_id={"tm": other_core},
            device_id_type=MESH,
        )

    def recv_att(h):
        return pltpu.make_async_remote_copy(
            src_ref=outgoing.at[h],
            dst_ref=attended.at[1 - group, h],
            send_sem=att_send_sem.at[h],
            recv_sem=att_recv_sem.at[h],
            device_id={"tm": other_core},
            device_id_type=MESH,
        )

    def send_own(h):
        for copy in load(h):
            copy.wait()
        for step in (-1, 1):
            pl.when(has_time[step])(lambda step=step: send_time(step, h).start())
        send_outer(0, h).start()
        if DIRECT_OWN:
            pl.when(jnp.logical_and(is_middle, straight(0, h)))(lambda: send_middle(0, h).start())

    for h in range(AHEAD):
        send_own(jnp.int32(h))

    exponent_scale = (HD ** (-0.5)) * LOG2E

    def attend(slot, h, first=False):
        scores = lax.dot_general(
            q_s[h], kv[slot, h, 0], (((1,), (1,)), ((), ())), preferred_element_type=jnp.float32
        )
        row_max = jnp.max(scores, axis=1, keepdims=True)
        if not first:
            old_max = m_s[h][:, :1]
            row_max = jnp.maximum(row_max, old_max)
        weights = jnp.exp2((scores - row_max) * exponent_scale)
        total = jnp.sum(weights, axis=1, keepdims=True)
        result = jnp.dot(weights.astype(jnp.bfloat16), kv[slot, h, 1], preferred_element_type=jnp.float32)
        if not first:
            keep = jnp.exp2((old_max - row_max) * exponent_scale)
            total = total + keep * l_s[h][:, :1]
            result = result + keep * acc_s[h]
        m_s[h] = jnp.broadcast_to(row_max, (rows, HD))
        l_s[h] = jnp.broadcast_to(total, (rows, HD))
        acc_s[h] = result

    def finish(h):
        acc_s[h] = acc_s[h] / l_s[h]
        attended[group, h] = acc_s[h, pl.ds(pl.multiple_of(group * half, 16), half), :].astype(jnp.bfloat16)
        outgoing[h] = acc_s[h, pl.ds(pl.multiple_of((1 - group) * half, 16), half), :].astype(jnp.bfloat16)

    def ready(h):
        return jnp.logical_and(h >= 0, h < heads)

    @pl.loop(0, heads + LAG_MIDDLE)
    def _(i):
        pl.when(i + AHEAD < heads)(lambda: send_own(i + AHEAD))

        @pl.when(jnp.logical_and(i < heads, is_edge))
        def _():
            arrive(own_slot + outer, i)
            pl.when(jnp.logical_not(straight(0, i)))(lambda: send_relay(0, i).start())

        @pl.when(jnp.logical_and(i < heads, is_hop))
        def _():
            for step in (-1, 1):
                arrive(hop_slot(step), i)
                send_hop(step, i).start()

        crossed = i - LAG_TIME

        @pl.when(ready(crossed))
        def _():
            for step in (-1, 1):

                @pl.when(has_time[step])
                def _():
                    arrive(slot_of(step, 0), crossed)
                    send_outer(step, crossed).start()
                    if DIRECT_CORNER:
                        pl.when(jnp.logical_and(is_middle, straight(step, crossed)))(
                            lambda: send_middle(step, crossed).start()
                        )

        back = i - LAG_CORNER

        @pl.when(jnp.logical_and(ready(back), is_edge))
        def _():
            for step in (-1, 1):

                @pl.when(has_time[step])
                def _():
                    arrive(slot_of(step, 0) + outer, back)
                    pl.when(jnp.logical_not(straight(step, back)))(lambda: send_relay(step, back).start())

        pl.when(i < heads)(lambda: attend(own_slot, i, first=True))

        @pl.when(ready(crossed))
        def _():
            for step in (-1, 1):
                pl.when(has_time[step])(lambda: attend(slot_of(step, 0), crossed))

        @pl.when(ready(back))
        def _():
            pl.when(is_middle)(lambda: arrive(own_slot + outer, back))
            attend(own_slot + outer, back)
            for step in (-1, 1):

                @pl.when(has_time[step])
                def _():
                    pl.when(is_middle)(lambda: arrive(slot_of(step, 0) + outer, back))
                    attend(slot_of(step, 0) + outer, back)

        last = i - LAG_MIDDLE

        @pl.when(last >= 1)
        def _():
            send_att(last - 1).start()

        @pl.when(last >= 0)
        def _():
            @pl.when(is_middle)
            def _():
                arrive(own_slot - outer, last)
                attend(own_slot - outer, last)
                for step in (-1, 1):

                    @pl.when(has_time[step])
                    def _():
                        arrive(slot_of(step, 0) - outer, last)
                        attend(slot_of(step, 0) - outer, last)

            finish(last)

    send_att(heads - 1).start()
    w_copy.wait()

    for h in range(heads):
        recv_att(h).wait_recv()

    width = out_ref.shape[1]
    chunk = 512
    lhs = jnp.concatenate([attended[part, h] for part in range(2) for h in range(heads)], axis=1)

    @pl.loop(0, width // chunk, unroll=True)
    def _(n):
        columns = pl.ds(pl.multiple_of(n * chunk, chunk), chunk)
        out_ref[:, columns] = jnp.dot(lhs, w_s[:, columns], preferred_element_type=jnp.float32).astype(
            out_ref.dtype
        )

    @pl.loop(0, heads)
    def _(h):
        send_att(h).wait_send()
        send_outer(0, h).wait_send()

        @pl.when(is_hop)
        def _():
            for step in (-1, 1):
                send_hop(step, h).wait_send()

        if DIRECT_OWN:
            pl.when(jnp.logical_and(is_middle, straight(0, h)))(lambda: send_middle(0, h).wait_send())
        pl.when(jnp.logical_and(is_edge, jnp.logical_not(straight(0, h))))(
            lambda: send_relay(0, h).wait_send()
        )
        for step in (-1, 1):

            @pl.when(has_time[step])
            def _():
                send_time(step, h).wait_send()
                send_outer(step, h).wait_send()
                if DIRECT_CORNER:
                    pl.when(jnp.logical_and(is_middle, straight(step, h)))(
                        lambda: send_middle(step, h).wait_send()
                    )
                pl.when(jnp.logical_and(is_edge, jnp.logical_not(straight(step, h))))(
                    lambda: send_relay(step, h).wait_send()
                )


def per_device(query_states, key_states, value_states, out_weight):
    rows, half_width = query_states.shape[1:]
    heads = half_width // HD
    depth, width = out_weight.shape
    time_count = lax.axis_size("tm") // (2 * TCOLS)
    return pl.pallas_call(
        functools.partial(kernel, time_count, heads),
        out_shape=jax.ShapeDtypeStruct((rows // 2, width), jnp.bfloat16),
        in_specs=[pl.BlockSpec(memory_space=pl.ANY)] * 4,
        out_specs=pl.BlockSpec(memory_space=pltpu.VMEM),
        scratch_shapes=[
            pltpu.VMEM((heads, rows, HD), jnp.bfloat16),
            pltpu.VMEM((11, heads, 2, rows, HD), jnp.bfloat16),
            pltpu.VMEM((depth, width), jnp.bfloat16),
            pltpu.VMEM((heads, rows, HD), jnp.float32),
            pltpu.VMEM((heads, rows, HD), jnp.float32),
            pltpu.VMEM((heads, rows, HD), jnp.float32),
            pltpu.VMEM((heads, rows // 2, HD), jnp.bfloat16),
            pltpu.VMEM((2, heads, rows // 2, HD), jnp.bfloat16),
            pltpu.SemaphoreType.DMA((3, heads)),
            pltpu.SemaphoreType.DMA,
            pltpu.SemaphoreType.DMA((13, heads)),
            pltpu.SemaphoreType.DMA((11, heads)),
            pltpu.SemaphoreType.DMA((heads,)),
            pltpu.SemaphoreType.DMA((heads,)),
        ],
        compiler_params=pltpu.CompilerParams(
            collective_id=0, has_side_effects=True, vmem_limit_bytes=56 * 1024 * 1024
        ),
    )(query_states, key_states, value_states, out_weight)


def solution(mesh):
    in_specs = (
        P(("parts", "tm"), None, None),
        P(("parts", "tm"), None, None),
        P(("parts", "tm"), None, None),
        P(),
    )
    out_specs = P(("parts", "tm"), None)
    return jax.shard_map(
        per_device, mesh=mesh, in_specs=in_specs, out_specs=out_specs, check_vma=False
    )
```
